512 devices in a mesh: seq: 64 (over z, x, y_hi), dp: 8 (over y_lo, core).
Axes of the slice: x: 4, y: 8 (y_hi: 2, y_lo: 4; y = y_hi * 4 + y_lo), z: 8, core: 2. Of those that a mesh axis runs over, the one named last changes fastest.
Arguments:
- query_in: bfloat16 [16384, 2048], P('seq', 'dp'), may hold values from -6 to 6
- key_in: bfloat16 [16384, 2048], P('seq', 'dp'), may hold values from -6 to 6
- value_in: bfloat16 [16384, 2048], P('seq', 'dp'), may hold values from -6 to 6
- filters: bfloat16 [16, 2048], P(None, 'dp'), may hold values from -0.125 to 0.125
- out_weight: bfloat16 [2048, 2048], P('dp'), may hold values from -0.125 to 0.125
- grad_mixed: bfloat16 [16384, 2048], P('seq', 'dp'), may hold values from -16 to 16
Outputs:
- grad_query: bfloat16 [16384, 2048], P('seq', 'dp')
- grad_key: bfloat16 [16384, 2048], P('seq', 'dp')
- grad_value: bfloat16 [16384, 2048], P('seq', 'dp')
- grad_weight: float32 [2048, 2048], P('dp', 'seq')
- grad_filters: float32 [16, 2048], P('dp', 'seq')
The draws below stay inside these ranges and needn't reach their ends.
All inputs are finite; a program needn't handle non-finite values.
Results may differ from the reference program's by a relative error of at most 0.0049.
Values may be sent and summed in bfloat16 or wider, within the bound.
No kernel may reach another device: no remote copies, remote signals or barrier semaphores. Data moves between devices by JAX's collectives and lax.ppermute only.
A program may use at most 64 MiB of HBM per device.

```python
import jax
import jax.numpy as jnp
from jax import lax

CHANNELS = 2048
NUM_FILTERS = 16
FILTER_LEN = 2048
TOKENS = 16384


def spiked(array, stream_key, source, target, shards_of, factor):
    owner, partner = [(jnp.arange(array.shape[dim]) // (array.shape[dim] // shards_of)).reshape([-1 if axis == dim else 1 for axis in range(array.ndim)]) for dim in (source, target)]
    chosen = jax.random.permutation(stream_key, shards_of)[partner]
    strong = (owner == chosen) | (owner == (partner + shards_of // 2) % shards_of)
    return jnp.where(strong, factor * array, array)


def steps_of(stream_key, shape, shards, least, high):
    gain, own = 1.0, jax.random.fold_in(stream_key, 6)
    for axis_at, blocks in shards:
        heights = jnp.exp(jax.random.uniform(jax.random.fold_in(own, axis_at), (blocks,), jnp.float32, least / len(shards), high / len(shards)))
        gain = gain * jnp.repeat(heights, shape[axis_at] // blocks).reshape([-1 if axis == axis_at else 1 for axis in range(len(shape))])
    return gain


def gaussian(key, dims, width, limit, shards=(), dtype=jnp.bfloat16):
    gain = steps_of(key, dims, shards, -0.22, 0.18) if shards else 1.0
    result = jax.random.normal(key, dims, jnp.float32) * width * gain
    return jnp.minimum(jnp.maximum(result, -limit), limit).astype(dtype)


def noise_with(stream_key, shape, spread, reach, pieces, heavy, held_as=jnp.bfloat16):
    values = spread * jax.random.normal(stream_key, shape, jnp.float32)
    if pieces:
        values = values * steps_of(stream_key, shape, pieces, -0.22, 0.18)
    return jnp.clip(spiked(values, jax.random.fold_in(stream_key, 3), *heavy), -reach, reach).astype(held_as)


def setup_inputs(seed: int = 0) -> dict:
    streams_of = jax.random.split(jax.random.key(seed), 7)
    return {
        "query_in": gaussian(streams_of[0], (TOKENS, CHANNELS), 1.0, 6.0, ((0, 64), (1, 8))),
        "key_in": gaussian(streams_of[1], (TOKENS, CHANNELS), 1.0, 6.0, ((0, 64), (1, 8))),
        "value_in": gaussian(streams_of[2], (TOKENS, CHANNELS), 1.0, 6.0, ((0, 64), (1, 8))),
        "filters": gaussian(streams_of[3], (NUM_FILTERS, FILTER_LEN), FILTER_LEN ** -0.5, 0.125, ((1, 8),)),
        "out_weight": gaussian(streams_of[4], (CHANNELS, CHANNELS), CHANNELS ** -0.5, 0.125, ((0, 8),)),
        "grad_mixed": noise_with(streams_of[5], (TOKENS, CHANNELS), 1.0, 16.0, ((0, 64), (1, 8)), (0, 1, 64, 4.0)),
    }


def causal_filter(signal, taps_row):
    length = signal.shape[0]
    period = length + taps_row.shape[0]
    spectrum = jnp.fft.rfft(signal, n=period, axis=0) * jnp.fft.rfft(taps_row, n=period)[:, None]
    return jnp.fft.irfft(spectrum, n=period, axis=0)[:length]


def lag_products(grads, inputs):
    length = grads.shape[0]
    period = length + FILTER_LEN
    spectrum = jnp.conj(jnp.fft.rfft(inputs, n=period, axis=0)) * jnp.fft.rfft(grads, n=period, axis=0)
    return jnp.sum(jnp.fft.irfft(spectrum, n=period, axis=0)[:FILTER_LEN], axis=1)


def reference(query_in, key_in, value_in, filters, out_weight, grad_mixed):
    group_width = CHANNELS // NUM_FILTERS
    products = (key_in.astype(jnp.float32) * value_in.astype(jnp.float32)).astype(jnp.bfloat16)
    taps_all = filters.astype(jnp.float32)

    def by_group(tensor):
        return tensor.astype(jnp.float32).reshape(TOKENS, NUM_FILTERS, group_width).transpose(1, 0, 2)

    def back_layout(tensor):
        return tensor.transpose(1, 0, 2).reshape(TOKENS, CHANNELS)

    def forward_group(member):
        return causal_filter(member[0], member[1])

    def backward_group(member):
        return causal_filter(member[0][::-1], member[1])[::-1]

    def filter_group(member):
        return lag_products(member[0], member[1])

    conv_out = back_layout(lax.map(forward_group, (by_group(products), taps_all)))
    gated = (query_in.astype(jnp.float32) * conv_out).astype(jnp.bfloat16)
    grad_gated = jnp.dot(grad_mixed, out_weight.T, preferred_element_type=jnp.float32)
    grad_query = (grad_gated * conv_out).astype(jnp.bfloat16)
    grad_conv = (grad_gated * query_in.astype(jnp.float32)).astype(jnp.bfloat16)
    grad_products = back_layout(lax.map(backward_group, (by_group(grad_conv), taps_all)))
    grad_key = (grad_products * value_in.astype(jnp.float32)).astype(jnp.bfloat16)
    grad_value = (grad_products * key_in.astype(jnp.float32)).astype(jnp.bfloat16)
    grad_filters = lax.map(filter_group, (by_group(grad_conv), by_group(products)))
    grad_weight = jnp.dot(gated.T, grad_mixed, preferred_element_type=jnp.float32)
    return (grad_query, grad_key, grad_value, grad_weight, grad_filters)
```

```python
import jax
import jax.numpy as jnp
from jax import lax
from jax.experimental import pallas as pl
from jax.experimental.pallas import tpu as pltpu
from jax.sharding import Mesh
from jax.sharding import PartitionSpec as P

Z, X, H, Y, C = 8, 4, 2, 4, 2
PLANE = ("x", "h")
SEQ = ("z", "x", "h")
BLOCKS = 8
TOK = 256
WIDTH = 256
SLICE = WIDTH // BLOCKS
MODEL = 2048
TAPS = 2048
FILTERS = 16
REACH = TAPS // TOK
SUB = 128
F32, BF16 = jnp.float32, jnp.bfloat16
NN = (((1,), (0,)), ((), ()))
NT = (((1,), (1,)), ((), ()))


def dot(a, b, dims):
    return lax.dot_general(a, b, dims, preferred_element_type=F32)


def flip(a):
    return a.astype(F32).T


def call(body, out_shapes, args, scalars=0, scratch=()):
    specs = [pl.BlockSpec(memory_space=pltpu.SMEM)] * scalars
    specs += [pl.BlockSpec(memory_space=pltpu.VMEM)] * (len(args) - scalars)
    outs = [pl.BlockSpec(memory_space=pltpu.VMEM)] * len(out_shapes)
    return pl.pallas_call(
        body,
        out_shape=[jax.ShapeDtypeStruct(s, t) for s, t in out_shapes],
        in_specs=specs,
        out_specs=outs,
        scratch_shapes=list(scratch),
        name=body.__name__,
    )(*args)


def prepare(q, k, v, gm, filters, pay, p_t, q_t):
    pay[0:WIDTH, :] = flip(gm[...]).astype(BF16)
    pay[WIDTH : WIDTH + FILTERS, :] = filters[...]
    p_t[...] = (k[...].astype(F32) * v[...].astype(F32)).T.astype(BF16)
    q_t[...] = flip(q[...]).astype(BF16)


def project(where, *refs):
    parts = refs[:8]
    weight, q_t, p_t, p_prev, gg_t, send, taps = refs[8:]
    acc = jnp.zeros((WIDTH, TOK), F32)
    rows = lax.broadcasted_iota(jnp.int32, (FILTERS, TOK), 0)
    for n in range(8):
        home = where[n]
        part = parts[n]
        columns = weight[:, pl.ds(pl.multiple_of(home * TOK, TOK), TOK)]
        acc += dot(columns, part[0:WIDTH, :], NN)
        mine = jnp.where(rows == where[8], part[WIDTH : WIDTH + FILTERS, :].astype(F32), 0.0)
        taps[pl.ds(home, 1), :] = jnp.sum(mine, axis=0, keepdims=True)
    gg_t[...] = acc
    gc = (acc * q_t[...].astype(F32)).astype(BF16)
    for r in range(BLOCKS):
        lo, hi = r * SLICE, (r + 1) * SLICE
        send[r, 0:SLICE, :] = p_t[lo:hi, :]
        send[r, SLICE : 2 * SLICE, :] = p_prev[lo:hi, :]
        send[r, 2 * SLICE : 3 * SLICE, :] = gc[lo:hi, :]


def forward(got, taps, band, conv, lags, gc_own, span, folded, sums):
    zero = jnp.zeros((1, SUB), F32)
    pieces = [zero]
    for n in range(TAPS // TOK):
        row = taps[n : n + 1, :]
        pieces += [row[:, 0:SUB], row[:, SUB:TOK]]
    pieces.append(zero)
    blank = jnp.zeros((SUB, SUB), BF16)
    for e in range(-1, 2 * REACH + 2):
        if 0 <= e <= 2 * REACH:
            line = jnp.concatenate([pieces[e], pieces[e + 1]], axis=1)
            wide = jnp.broadcast_to(line, (SUB, 2 * SUB))
            tile = pltpu.roll(wide, 0, 1, stride=1, stride_axis=0)[:, SUB:].astype(BF16)
        else:
            tile = blank
        for d in range(REACH + 1):
            for jb in range(2):
                for ib in range(2):
                    if 2 * d + ib - jb == e:
                        band[d * TOK + jb * SUB : d * TOK + (jb + 1) * SUB, ib * SUB : (ib + 1) * SUB] = tile
    for b in range(BLOCKS):
        span[b * SLICE : (b + 1) * SLICE, :] = got[b, SLICE : 2 * SLICE, :]
        span[WIDTH + b * SLICE : WIDTH + (b + 1) * SLICE, :] = got[b, 0:SLICE, :]
        gc_own[b * SLICE : (b + 1) * SLICE, :] = got[b, 2 * SLICE : 3 * SLICE, :]
    acc = jnp.zeros((WIDTH, TOK), F32)
    for d in range(REACH + 1):
        low = (BLOCKS - d) * SLICE
        acc += dot(span[low : low + WIDTH, :], band[d * TOK : (d + 1) * TOK, :], NN)
    conv[...] = acc.astype(BF16)
    r = lax.broadcasted_iota(jnp.int32, (TOK, TOK), 0)
    c = lax.broadcasted_iota(jnp.int32, (TOK, TOK), 1)
    mirror = jnp.where((r // SUB == c // SUB) & (r % SUB + c % SUB == SUB - 1), 1.0, 0.0).astype(BF16)
    folded[...] = dot(span[...], mirror, NN).astype(BF16)
    grads = flip(gc_own[...]).astype(BF16)
    sums[...] = jnp.zeros(sums.shape, F32)
    for d in range(REACH + 1):
        low = (BLOCKS - d) * SLICE
        m = dot(grads, folded[low : low + WIDTH, :], NN)
        for ib in range(2):
            for jb in range(2):
                e = 2 * d + ib - jb
                if 0 <= e <= 2 * REACH:
                    sums[e] = sums[e] + m[ib * SUB : (ib + 1) * SUB, jb * SUB : (jb + 1) * SUB]
    lines = []
    for e in range(2 * REACH + 1):
        wide = jnp.concatenate([sums[e], jnp.zeros((SUB, SUB), F32)], axis=1)
        lines.append(jnp.sum(pltpu.roll(wide, 1, 1, stride=1, stride_axis=0), axis=0, keepdims=True))
    for e in range(2 * REACH):
        lags[e : e + 1, :] = lines[e][:, SUB:] + lines[e + 1][:, 0:SUB]


def backward(gc_own, gc_next, band, conv, send, span):
    span[0:WIDTH, :] = gc_own[...]
    span[WIDTH : 2 * WIDTH, :] = gc_next[...]
    acc = jnp.zeros((WIDTH, TOK), F32)
    for d in range(REACH + 1):
        acc += dot(span[d * SLICE : d * SLICE + WIDTH, :], band[d * TOK : (d + 1) * TOK, :], NT)
    gp = acc.astype(BF16)
    for b in range(BLOCKS):
        lo, hi = b * SLICE, (b + 1) * SLICE
        send[b, 0:SLICE, :] = conv[lo:hi, :]
        send[b, SLICE : 2 * SLICE, :] = gp[lo:hi, :]


def finish(where, *refs):
    parts = refs[:8]
    got, gg_t, q_t, k, v, lags, gq, gk, gv, send, part_sum = refs[8:]
    conv = jnp.concatenate([got[r, 0:SLICE, :] for r in range(BLOCKS)], axis=0).astype(F32)
    gp = jnp.concatenate([got[r, SLICE : 2 * SLICE, :] for r in range(BLOCKS)], axis=0).astype(F32).T
    gq[...] = (gg_t[...] * conv).T.astype(BF16)
    gk[...] = (gp * v[...].astype(F32)).astype(BF16)
    gv[...] = (gp * k[...].astype(F32)).astype(BF16)
    gated = (q_t[...].astype(F32) * conv).astype(BF16)
    per = TOK // 32
    for n in range(8):
        part_sum[...] = dot(parts[n][0:WIDTH, :], gated, NT).astype(BF16)
        home = where[n]
        for s in range(per):
            send[home * per + s, 0:32, :] = part_sum[s * 32 : (s + 1) * 32, :]
    rows = lax.broadcasted_iota(jnp.int32, (8, WIDTH), 0)
    mine = where[9]
    for e in range(16):
        line = lags[e : e + 1, :]
        for s in range(4):
            cut = line[:, s * 32 : (s + 1) * 32]
            wide = jnp.concatenate([cut, jnp.zeros((1, WIDTH - 32), F32)], axis=1)
            top = wide.astype(BF16)
            low = wide - top.astype(F32)
            tile = jnp.where(rows == mine, top.astype(F32), jnp.where(rows == mine + 2, low, 0.0))
            send[e * 4 + s, 32:40, :] = tile.astype(BF16)


def collect(got, gw, gf):
    acc = jnp.zeros((40, WIDTH), F32)
    for s in range(64):
        acc += got[s].astype(F32)
    gw[...] = acc[0:32, :].T
    gf[...] = acc[32:34, 0:32] + acc[34:36, 0:32]


def shift(block, axis, distance, size):
    return lax.ppermute(block, axis, [(i, i + distance) for i in range(size) if 0 <= i + distance < size])


def per_device(q, k, v, filters, weight, gm):
    y, c = lax.axis_index("y"), lax.axis_index("c")
    own_filter = lax.axis_index("x") // 2
    pay, p_t, q_t = call(
        prepare, [((WIDTH + FILTERS, TOK), BF16), ((WIDTH, TOK), BF16), ((WIDTH, TOK), BF16)], (q, k, v, gm, filters)
    )
    line = [pay] + [lax.ppermute(pay, "y", [(i, (i + n) % Y) for i in range(Y)]) for n in range(1, Y)]
    other = [lax.ppermute(part, "c", [(0, 1), (1, 0)]) for part in line]
    parts = line + other
    homes = [((y - n) % Y) * C + c for n in range(Y)] + [((y - n) % Y) * C + 1 - c for n in range(Y)]
    where = jnp.stack(homes + [(y * C + c) * 2 + own_filter, own_filter]).astype(jnp.int32)
    p_prev = shift(p_t, "z", 1, Z)
    gg_t, send, taps = call(
        project,
        [((WIDTH, TOK), F32), ((BLOCKS, 3 * SLICE, TOK), BF16), ((TAPS // TOK, TOK), F32)],
        (where, *parts, weight, q_t, p_t, p_prev),
        scalars=1,
    )
    got = lax.all_to_all(send, PLANE, 0, 0, tiled=True)
    gc_early = got[:, 2 * SLICE :, :].reshape(WIDTH, TOK)
    gc_next = shift(gc_early, "z", -1, Z)
    band, conv, lags, gc_own = call(
        forward,
        [(((REACH + 1) * TOK, TOK), BF16), ((WIDTH, TOK), BF16), ((16, SUB), F32), ((WIDTH, TOK), BF16)],
        (got, taps),
        scratch=(
            pltpu.VMEM((2 * WIDTH, TOK), BF16),
            pltpu.VMEM((2 * WIDTH, TOK), BF16),
            pltpu.VMEM((2 * REACH + 1, SUB, SUB), F32),
        ),
    )
    (send,) = call(
        backward,
        [((BLOCKS, 2 * SLICE, TOK), BF16)],
        (gc_own, gc_next, band, conv),
        scratch=(pltpu.VMEM((2 * WIDTH, TOK), BF16),),
    )
    got = lax.all_to_all(send, PLANE, 0, 0, tiled=True)
    gq, gk, gv, send = call(
        finish,
        [((TOK, WIDTH), BF16)] * 3 + [((64, 40, WIDTH), BF16)],
        (where, *parts, got, gg_t, q_t, k, v, lags),
        scalars=1,
        scratch=(pltpu.VMEM((TOK, WIDTH), BF16),),
    )
    got = lax.all_to_all(send, SEQ, 0, 0, tiled=True)
    gw, gf = call(collect, [((WIDTH, 32), F32), ((2, 32), F32)], (got,))
    return gq, gk, gv, gw, gf


def solution(mesh):
    fine = Mesh(mesh.devices.reshape(Z, X, H, Y, C), ("z", "x", "h", "y", "c"))
    seq, dp = SEQ, ("y", "c")
    in_specs = (P(seq, dp), P(seq, dp), P(seq, dp), P(None, dp), P(dp, None), P(seq, dp))
    out_specs = (P(seq, dp), P(seq, dp), P(seq, dp), P(dp, seq), P(dp, seq))
    return jax.shard_map(per_device, mesh=fine, in_specs=in_specs, out_specs=out_specs, check_vma=False)
```

```python
import jax
import jax.numpy as jnp
from jax import lax
from jax.experimental import pallas as pl
from jax.experimental.pallas import tpu as pltpu
from jax.sharding import Mesh
from jax.sharding import PartitionSpec as P

Z, X, H, Y, C = 8, 4, 2, 4, 2
PLANE = ("x", "h")
SEQ = ("z", "x", "h")
BLOCKS = 8
TOK = 256
WIDTH = 256
SLICE = WIDTH // BLOCKS
MODEL = 2048
TAPS = 2048
FILTERS = 16
REACH = TAPS // TOK
SUB = 128
PAY = WIDTH + FILTERS
ROWS = SLICE + 8
F32, BF16 = jnp.float32, jnp.bfloat16
NN = (((1,), (0,)), ((), ()))
NT = (((1,), (1,)), ((), ()))


def dot(a, b, dims):
    return lax.dot_general(a, b, dims, preferred_element_type=F32)


def flip(a):
    return a.astype(F32).T


def call(body, out_shapes, args, scalars=0, scratch=()):
    specs = [pl.BlockSpec(memory_space=pltpu.SMEM)] * scalars
    specs += [pl.BlockSpec(memory_space=pltpu.VMEM)] * (len(args) - scalars)
    outs = [pl.BlockSpec(memory_space=pltpu.VMEM)] * len(out_shapes)
    return pl.pallas_call(
        body,
        out_shape=[jax.ShapeDtypeStruct(s, t) for s, t in out_shapes],
        in_specs=specs,
        out_specs=outs,
        scratch_shapes=list(scratch),
        name=body.__name__,
    )(*args)


def prepare(q, k, v, gm, filters, pay, p_t, q_t):
    pay[0:WIDTH, :] = flip(gm[...]).astype(BF16)
    pay[WIDTH:PAY, :] = filters[...]
    p_t[...] = (k[...].astype(F32) * v[...].astype(F32)).T.astype(BF16)
    q_t[...] = flip(q[...]).astype(BF16)


def fill_band(band, taps):
    zero = jnp.zeros((1, SUB), F32)
    pieces = [zero]
    for n in range(TAPS // TOK):
        row = taps[n : n + 1, :]
        pieces += [row[:, 0:SUB], row[:, SUB:TOK]]
    pieces.append(zero)
    for e in range(-1, 2 * REACH + 2):
        if 0 <= e <= 2 * REACH:
            line = jnp.concatenate([pieces[e], pieces[e + 1]], axis=1)
            wide = jnp.broadcast_to(line, (SUB, 2 * SUB))
            tile = pltpu.roll(wide, 0, 1, stride=1, stride_axis=0)[:, SUB:].astype(BF16)
        else:
            tile = jnp.zeros((SUB, SUB), BF16)
        for d in range(REACH + 1):
            for jb in range(2):
                for ib in range(2):
                    if 2 * d + ib - jb == e:
                        band[d * TOK + jb * SUB : d * TOK + (jb + 1) * SUB, ib * SUB : (ib + 1) * SUB] = tile


def project(where, own, other, weight, q_t, p_got, p_prev, gg_t, send, band, taps, span):
    acc = jnp.zeros((WIDTH, TOK), F32)
    rows = lax.broadcasted_iota(jnp.int32, (FILTERS, TOK), 0)
    for n in range(8):
        home = where[n]
        part, low = (own, n * PAY) if n < Y else (other, (n - Y) * PAY)
        columns = weight[:, pl.ds(pl.multiple_of(home * TOK, TOK), TOK)]
        acc += dot(columns, part[low : low + WIDTH, :], NN)
        mine = jnp.where(rows == where[8], part[low + WIDTH : low + PAY, :].astype(F32), 0.0)
        taps[pl.ds(home, 1), :] = jnp.sum(mine, axis=0, keepdims=True)
    gg_t[...] = acc
    gc = (acc * q_t[...].astype(F32)).astype(BF16)
    fill_band(band, taps)
    span[0:WIDTH, :] = p_prev[...]
    for b in range(BLOCKS):
        span[WIDTH + b * SLICE : WIDTH + (b + 1) * SLICE, :] = p_got[b]
    acc = jnp.zeros((WIDTH, TOK), F32)
    for d in range(REACH + 1):
        low = (BLOCKS - d) * SLICE
        acc += dot(span[low : low + WIDTH, :], band[d * TOK : (d + 1) * TOK, :], NN)
    conv = acc.astype(BF16)
    for r in range(BLOCKS):
        lo, hi = r * SLICE, (r + 1) * SLICE
        send[r, 0:SLICE, :] = conv[lo:hi, :]
        send[r, SLICE : 2 * SLICE, :] = gc[lo:hi, :]


def conv_of(got):
    return jnp.concatenate([got[r, 0:SLICE, :] for r in range(BLOCKS)], axis=0).astype(F32)


def weigh(where, own, other, got, q_t, send, part_sum):
    gated = (q_t[...].astype(F32) * conv_of(got)).astype(BF16)
    for n in range(8):
        part, low = (own, n * PAY) if n < Y else (other, (n - Y) * PAY)
        part_sum[...] = dot(part[low : low + WIDTH, :], gated, NT).astype(BF16)
        at = pl.multiple_of(where[n] * SLICE, SLICE)
        for x in range(X):
            for h in range(H):
                lo = (x * H + h) * SLICE
                send[x, pl.ds(h * WIDTH + at, SLICE), :] = part_sum[lo : lo + SLICE, :]


def backward(got, gc_next, band, p_got, p_prev, gg_t, send, gq, ahead, span, folded, sums):
    gq[...] = (gg_t[...] * conv_of(got)).T.astype(BF16)
    span[0:WIDTH, :] = p_prev[...]
    for b in range(BLOCKS):
        span[WIDTH + b * SLICE : WIDTH + (b + 1) * SLICE, :] = p_got[b]
        ahead[b * SLICE : (b + 1) * SLICE, :] = got[b, SLICE : 2 * SLICE, :]
    ahead[WIDTH : 2 * WIDTH, :] = gc_next[...]
    acc = jnp.zeros((WIDTH, TOK), F32)
    for d in range(REACH + 1):
        acc += dot(ahead[d * SLICE : d * SLICE + WIDTH, :], band[d * TOK : (d + 1) * TOK, :], NT)
    gp = acc.astype(BF16)
    for b in range(BLOCKS):
        send[b, 0:SLICE, :] = gp[b * SLICE : (b + 1) * SLICE, :]
    r = lax.broadcasted_iota(jnp.int32, (TOK, TOK), 0)
    c = lax.broadcasted_iota(jnp.int32, (TOK, TOK), 1)
    mirror = jnp.where((r // SUB == c // SUB) & (r % SUB + c % SUB == SUB - 1), 1.0, 0.0).astype(BF16)
    folded[...] = dot(span[...], mirror, NN).astype(BF16)
    grads = flip(ahead[0:WIDTH, :]).astype(BF16)
    sums[...] = jnp.zeros(sums.shape, F32)
    for d in range(REACH + 1):
        low = (BLOCKS - d) * SLICE
        m = dot(grads, folded[low : low + WIDTH, :], NN)
        for ib in range(2):
            for jb in range(2):
                e = 2 * d + ib - jb
                if 0 <= e <= 2 * REACH:
                    sums[e] = sums[e] + m[ib * SUB : (ib + 1) * SUB, jb * SUB : (jb + 1) * SUB]
    lines = []
    for e in range(2 * REACH + 1):
        wide = jnp.concatenate([sums[e], jnp.zeros((SUB, SUB), F32)], axis=1)
        lines.append(jnp.sum(pltpu.roll(wide, 1, 1, stride=1, stride_axis=0), axis=0, keepdims=True))
    for odd in range(2):
        lags = [lines[e][:, SUB:] + lines[e + 1][:, 0:SUB] for e in range(odd, 2 * REACH, 2)]
        both = split(jnp.concatenate(lags, axis=0))
        for b in range(BLOCKS // 2):
            send[odd * (BLOCKS // 2) + b, SLICE:ROWS, :] = both


def split(a):
    high = a.astype(BF16)
    return jnp.concatenate([high, (a - high.astype(F32)).astype(BF16)], axis=1)


def sum_x(where, got, keep, away):
    acc = [got[0, h * WIDTH : (h + 1) * WIDTH, :].astype(F32) for h in range(H)]
    for x in range(1, X):
        acc = [acc[h] + got[x, h * WIDTH : (h + 1) * WIDTH, :].astype(F32) for h in range(H)]
    first = where[10] == 0
    keep[...] = jnp.where(first, acc[0], acc[1])
    away[...] = jnp.where(first, acc[1], acc[0]).astype(BF16)


def sum_h(got, keep, came, send):
    total = (keep[...] + came[...].astype(F32)).astype(BF16)
    lags = []
    for f in range(2):
        acc = jnp.zeros((8, 2 * SUB), F32)
        for r in range(BLOCKS // 2):
            acc += got[f * (BLOCKS // 2) + r, SLICE:ROWS, :].astype(F32)
        lags.append(split(acc[:, 0:SUB] + acc[:, SUB:]).astype(F32))
    rows = lax.broadcasted_iota(jnp.int32, (8, WIDTH), 0)
    for z in range(Z):
        send[z, 0:SLICE, :] = total[z * SLICE : (z + 1) * SLICE, :]
        tile = jnp.where(rows == 0, lags[0][z : z + 1, :], jnp.where(rows == 1, lags[1][z : z + 1, :], 0.0))
        send[z, SLICE:ROWS, :] = tile.astype(BF16)


def scale(got, k, v, gk, gv):
    gp = jnp.concatenate([got[r, 0:SLICE, :] for r in range(BLOCKS)], axis=0).astype(F32).T
    gk[...] = (gp * v[...].astype(F32)).astype(BF16)
    gv[...] = (gp * k[...].astype(F32)).astype(BF16)


def collect(where, got, gw_t, gf):
    acc = jnp.zeros((ROWS, WIDTH), F32)
    for z in range(Z):
        acc += got[z].astype(F32)
    gw_t[...] = acc[0:SLICE, :]
    lags = acc[SLICE : SLICE + 2, 0:SUB] + acc[SLICE : SLICE + 2, SUB:]
    out = jnp.zeros((2, SLICE), F32)
    for n in range(4):
        out += jnp.where(where[11] == n, lags[:, n * SLICE : (n + 1) * SLICE], 0.0)
    gf[...] = out


def shift(block, axis, distance, size):
    return lax.ppermute(block, axis, [(i, i + distance) for i in range(size) if 0 <= i + distance < size])


def per_device(q, k, v, filters, weight, gm):
    y, c, x, h = (lax.axis_index(a) for a in ("y", "c", "x", "h"))
    own_filter = x // 2
    square = (WIDTH, TOK)
    pay, p_t, q_t = call(prepare, [((PAY, TOK), BF16), (square, BF16), (square, BF16)], (q, k, v, gm, filters))
    homes = [((y - n) % Y) * C + c for n in range(Y)] + [((y - n) % Y) * C + 1 - c for n in range(Y)]
    where = jnp.stack(homes + [(y * C + c) * 2 + own_filter, own_filter, h, (x * H + h) % 4]).astype(jnp.int32)
    line = [pay] + [lax.ppermute(pay, "y", [(i, (i + n) % Y) for i in range(Y)]) for n in range(1, Y)]
    p_got = lax.all_to_all(p_t.reshape(BLOCKS, SLICE, TOK), PLANE, 0, 0, tiled=True)
    own = jnp.concatenate(line, axis=0)
    other = lax.ppermute(own, "c", [(0, 1), (1, 0)])
    p_prev = shift(p_got.reshape(square), "z", 1, Z)
    gg_t, send, band = call(
        project,
        [(square, F32), ((BLOCKS, 2 * SLICE, TOK), BF16), (((REACH + 1) * TOK, TOK), BF16)],
        (where, own, other, weight, q_t, p_got, p_prev),
        scalars=1,
        scratch=(pltpu.VMEM((TAPS // TOK, TOK), F32), pltpu.VMEM((2 * WIDTH, TOK), BF16)),
    )
    got = lax.all_to_all(send, PLANE, 0, 0, tiled=True)
    gc_next = shift(got[:, SLICE:, :].reshape(square), "z", -1, Z)
    (send,) = call(
        weigh,
        [((X, H * WIDTH, WIDTH), BF16)],
        (where, own, other, got, q_t),
        scalars=1,
        scratch=(pltpu.VMEM((TOK, WIDTH), BF16),),
    )
    got_x = lax.all_to_all(send, "x", 0, 0, tiled=True)
    send, gq = call(
        backward,
        [((BLOCKS, ROWS, TOK), BF16), (square, BF16)],
        (got, gc_next, band, p_got, p_prev, gg_t),
        scratch=(
            pltpu.VMEM((2 * WIDTH, TOK), BF16),
            pltpu.VMEM((2 * WIDTH, TOK), BF16),
            pltpu.VMEM((2 * WIDTH, TOK), BF16),
            pltpu.VMEM((2 * REACH + 1, SUB, SUB), F32),
        ),
    )
    keep, away = call(sum_x, [(square, F32), (square, BF16)], (where, got_x), scalars=1)
    came = lax.ppermute(away, "h", [(0, 1), (1, 0)])
    got = lax.all_to_all(send, PLANE, 0, 0, tiled=True)
    (send,) = call(sum_h, [((Z, ROWS, WIDTH), BF16)], (got, keep, came))
    got_z = lax.all_to_all(send, "z", 0, 0, tiled=True)
    gk, gv = call(scale, [(square, BF16)] * 2, (got, k, v))
    gw_t, gf = call(collect, [((SLICE, WIDTH), F32), ((2, SLICE), F32)], (where, got_z), scalars=1)
    return gq, gk, gv, gw_t.T, gf


def solution(mesh):
    fine = Mesh(mesh.devices.reshape(Z, X, H, Y, C), ("z", "x", "h", "y", "c"))
    seq, dp = SEQ, ("y", "c")
    in_specs = (P(seq, dp), P(seq, dp), P(seq, dp), P(None, dp), P(dp, None), P(seq, dp))
    out_specs = (P(seq, dp), P(seq, dp), P(seq, dp), P(dp, seq), P(dp, seq))
    return jax.shard_map(per_device, mesh=fine, in_specs=in_specs, out_specs=out_specs, check_vma=False)
```
